32 devices in a mesh: parts: 2 (over y), seq: 4 (over z), heads: 2 (over x), sub: 2 (over core).
Axes of the slice: x: 2, y: 2, z: 4, core: 2. Of those that a mesh axis runs over, the one named last changes fastest.
Arguments:
- queries: bfloat16 [8192, 4096], P(('parts', 'seq', 'sub'), 'heads'), parts along dimension 0, as said below
- keys: bfloat16 [8192, 4096], P(('parts', 'seq', 'sub'), 'heads'), parts along dimension 0, as said below
- values: bfloat16 [8192, 4096], P(('parts', 'seq', 'sub'), 'heads'), parts along dimension 0, may hold values from -6 to 6
- half_width: int32 [32], replicated, may hold values from 128 to 512, as said below
- valid_length: int32 [2], P('parts'), parts along dimension 0, may hold values from 3328 to 4096
- out_weight: bfloat16 [4096, 4096], P('heads', 'sub'), may hold values from -1.5 to 1.5
Outputs:
- projected: bfloat16 [8192, 4096], P(('parts', 'seq', 'sub'), 'heads'), parts along dimension 0
The draws below stay inside these ranges and needn't reach their ends.
There are 2 independent parts, one for each index of `parts`. The reference program is written for one: setup_inputs(seed, part) draws one part's arguments, and reference() takes and returns one part's arrays. A program takes and returns all parts, laid end to end along the dimension named above; an argument that names none is the same for every part. Nothing has to cross between parts.
Inputs may be any that keep to these rules, and one draw needn't show every extreme that they name: queries with 32 heads of 128 entries side by side. keys with 32 heads of 128 entries side by side. `half_width`: some head's half-width is exactly 512.
All inputs are finite; a program needn't handle non-finite values.
Results may differ from the reference program's by a relative error of at most 0.014.
Values may be sent and summed in bfloat16 or wider, within the bound.
A program may use at most 192 MiB of HBM per device.

```python
import math
import jax
import jax.numpy as jnp
from jax import lax

H = 32
HD = 128
D = 4096
TOK_DEV = 512
TOKENS = 4096
N_HEADS = 2


def common_draw(key):
    total_width = H * HD
    query_raw = jax.random.normal(jax.random.fold_in(key, 11), (TOKENS, total_width), jnp.float32)
    key_raw = jax.random.normal(jax.random.fold_in(key, 12), (TOKENS, total_width), jnp.float32)
    return (query_raw, key_raw)


def draw_queries(key, part):
    return common_draw(key)[0].astype(jnp.bfloat16)


def draw_keys(key, part):
    return common_draw(key)[1].astype(jnp.bfloat16)


def draw_half_width(key, part):
    widths = jax.random.randint(jax.random.fold_in(key, 21), (H,), TOK_DEV // 4, TOK_DEV + 1).astype(jnp.int32)
    order = jax.random.permutation(jax.random.fold_in(key, 22), H)
    widths = widths.at[order[0]].set(TOK_DEV)
    widths = widths.at[order[1]].set(TOK_DEV // 4)
    return widths.astype(jnp.int32)


def with_spikes(array, own_key, source, target, shards_of, factor):
    owner, partner = [(jnp.arange(array.shape[position]) // (array.shape[position] // shards_of)).reshape([-1 if axis == position else 1 for axis in range(array.ndim)]) for position in (source, target)]
    chosen = jax.random.permutation(own_key, shards_of)[partner]
    strong = (owner == chosen) | (owner == (partner + shards_of // 2) % shards_of)
    return jnp.where(strong, factor * array, array)


def block_levels(rng, dims, cuts, least, high):
    def one(axis_at, blocks):
        heights = jax.random.uniform(jax.random.fold_in(jax.random.fold_in(rng, 6), axis_at), (blocks,), jnp.float32, least / len(cuts), high / len(cuts))
        return jnp.repeat(jnp.exp(heights), dims[axis_at] // blocks).reshape((-1,) + (1,) * (len(dims) - axis_at - 1))

    gain = one(*cuts[0])
    for cut in cuts[1:]:
        gain = gain * one(*cut)
    return gain


def normal_values(rng, shape, spread, most, cuts=(), kind=jnp.bfloat16):
    drawn = jax.random.normal(rng, shape, jnp.float32) * spread
    if len(cuts) > 0:
        drawn = block_levels(rng, shape, cuts, -0.22, 0.18) * drawn
    return jnp.clip(drawn, min=-most, max=most).astype(kind)


def gaussian_with(stream_key, dims, spread, reach, shards, heavy, held_as=jnp.bfloat16):
    array = spread * jax.random.normal(stream_key, dims, jnp.float32)
    if shards:
        array = array * block_levels(stream_key, dims, shards, -0.22, 0.18)
    return jnp.clip(with_spikes(array, jax.random.fold_in(stream_key, 3), *heavy), -reach, reach).astype(held_as)


def setup_inputs(seed: int = 0, part: int = 0) -> dict:
    splits = jax.random.split(jax.random.key(seed), 7)
    own_keys = jax.random.split(jax.random.fold_in(splits[6], part), 7)
    return {
        "queries": draw_queries(jax.random.fold_in(jax.random.fold_in(splits[6], part), 71), part),
        "keys": draw_keys(jax.random.fold_in(jax.random.fold_in(splits[6], part), 71), part),
        "values": normal_values(own_keys[2], (TOKENS, H * HD), 1.0, 6.0, ((0, 8), (1, 2))),
        "half_width": draw_half_width(jax.random.fold_in(splits[6], 71), part),
        "valid_length": jax.random.randint(own_keys[4], (1,), TOKENS - TOK_DEV - TOK_DEV // 2, TOKENS + 1).astype(jnp.int32),
        "out_weight": gaussian_with(splits[5], (H * HD, D), H ** -0.5, 1.5, ((0, 2), (1, 2)), (0, 1, 2, 2.0)),
    }


def reference(queries, keys, values, half_width, valid_length, out_weight):
    heads_group = H // N_HEADS
    query_heads = queries.reshape(TOKENS, H, HD)
    key_heads = keys.reshape(TOKENS, H, HD)
    value_heads = values.reshape(TOKENS, H, HD)
    padding = jnp.zeros((TOK_DEV, H, HD), jnp.bfloat16)
    key_padded = jnp.concatenate([padding, key_heads, padding], axis=0)
    value_padded = jnp.concatenate([padding, value_heads, padding], axis=0)
    length_end = valid_length[0]
    score_scale = 1.0 / math.sqrt(HD)
    block_count = TOKENS // TOK_DEV

    def one_block(block_index):
        first_row = block_index * TOK_DEV
        query_block = lax.dynamic_slice_in_dim(query_heads, first_row, TOK_DEV, 0)
        key_block = lax.dynamic_slice_in_dim(key_padded, first_row, 3 * TOK_DEV, 0)
        value_block = lax.dynamic_slice_in_dim(value_padded, first_row, 3 * TOK_DEV, 0)
        query_pos = first_row + jnp.arange(TOK_DEV, dtype=jnp.int32)
        key_pos = first_row - TOK_DEV + jnp.arange(3 * TOK_DEV, dtype=jnp.int32)
        distance = jnp.abs(query_pos[:, None] - key_pos[None, :])
        key_fine = (key_pos >= 0) & (key_pos < length_end)
        opened = (distance[None, :, :] <= half_width[:, None, None]) & key_fine[None, None, :]
        scores = jnp.einsum('ihd,jhd->hij', query_block.astype(jnp.float32), key_block.astype(jnp.float32)) * score_scale
        highest = lax.optimization_barrier(jnp.max(jnp.where(opened, scores, jnp.float32(-1e+30)), axis=2, keepdims=True))
        weights = jnp.where(opened, jnp.exp(scores - highest), jnp.float32(0.0))
        totals = lax.optimization_barrier(jnp.sum(weights, axis=2))
        weights_low = lax.optimization_barrier(weights.astype(jnp.bfloat16))
        numerator = jnp.einsum('hij,jhd->ihd', weights_low.astype(jnp.float32), value_block.astype(jnp.float32))
        valid_rows = query_pos < length_end
        safe_totals = jnp.where(valid_rows[None, :], totals, jnp.float32(1.0))
        attended_block = numerator / safe_totals.T[:, :, None]
        attended_block = jnp.where(valid_rows[:, None, None], attended_block, jnp.float32(0.0))
        return attended_block.reshape(TOK_DEV, H * HD).astype(jnp.bfloat16)
    attended = lax.map(one_block, jnp.arange(block_count, dtype=jnp.int32)).reshape(TOKENS, H * HD)
    group_width = heads_group * HD

    def add_group(running, group_index):
        columns = lax.dynamic_slice_in_dim(attended, group_index * group_width, group_width, 1)
        weight_rows = lax.dynamic_slice_in_dim(out_weight, group_index * group_width, group_width, 0)
        group_sum = jnp.dot(columns, weight_rows, preferred_element_type=jnp.float32).astype(jnp.bfloat16)
        group_sum = lax.optimization_barrier(group_sum)
        return (running + group_sum.astype(jnp.float32), None)
    summed, unused = lax.scan(add_group, jnp.zeros((TOKENS, D), jnp.float32), jnp.arange(H // heads_group, dtype=jnp.int32))
    return summed.astype(jnp.bfloat16)
```

```python
import math

import jax
import jax.numpy as jnp
from jax import lax
from jax.experimental import pallas as pl
from jax.experimental.pallas import tpu as pltpu
from jax.sharding import PartitionSpec as P

HD = 128
R = 64
CHUNK = 128
PARTS = 4
G = 2
CLOSED = -1e30
FAR = 1 << 20
EXP2_SCALE = math.log2(math.e) / math.sqrt(HD)
MESH = pl.DeviceIdType.MESH


def kernel(
    half_width,
    valid_length,
    q_hbm,
    k_hbm,
    v_hbm,
    w_hbm,
    out_ref,
    qbuf,
    kbuf,
    vbuf,
    zk,
    zv,
    kt,
    wbuf,
    distance,
    attended,
    terms,
    own_in,
    x_in,
    scores,
    tops,
    weights,
    local_sem,
    z_send,
    z_recv,
    c_send,
    c_recv,
    a_send,
    a_recv,
    o_send,
    o_recv,
    x_send,
    x_recv,
):
    rows, width = qbuf.shape
    heads_here = width // HD
    steps = rows // R
    blocks = 2 * rows // CHUNK + 1
    span = blocks * CHUNK
    cols = width // PARTS
    seq = lax.axis_index("seq")
    group = lax.axis_index("heads")
    sub = lax.axis_index("sub")
    has_z = jnp.where(sub == 0, seq > 0, seq < lax.axis_size("seq") - 1)
    sends_x = sub == 1 - group
    chip_peer = {"sub": 1 - sub}
    z_peer = {"seq": seq + 2 * sub - 1, "sub": 1 - sub}
    first = (seq * 2 + sub) * rows
    length_end = valid_length[0]

    barrier = pltpu.get_barrier_semaphore()
    pl.semaphore_signal(barrier, inc=1, device_id=chip_peer, device_id_type=MESH)
    for core in range(2):
        pl.semaphore_signal(
            barrier, inc=1, device_id={"heads": 1 - group, "sub": core}, device_id_type=MESH
        )

    @pl.when(has_z)
    def _():
        pl.semaphore_signal(barrier, inc=1, device_id=z_peer, device_id_type=MESH)

    own_rows = pl.ds(rows, rows)
    z_rows = pl.ds(pl.multiple_of(2 * rows * sub, rows), rows)
    locals_ = [
        pltpu.make_async_copy(k_hbm, kbuf.at[own_rows], local_sem.at[0]),
        pltpu.make_async_copy(q_hbm, qbuf, local_sem.at[1]),
        pltpu.make_async_copy(v_hbm, vbuf.at[own_rows], local_sem.at[2]),
        pltpu.make_async_copy(w_hbm, wbuf, local_sem.at[3]),
    ]
    for copy in locals_:
        copy.start()
    pl.semaphore_wait(barrier, 3 + has_z.astype(jnp.int32))

    def z_copies(step):
        start = jnp.where(sub == 0, step * R, rows - R - step * R)
        source = pl.ds(pl.multiple_of(start, R), R)
        landing = pl.ds(pl.multiple_of(step * R, R), R)
        return [
            pltpu.make_async_remote_copy(
                src_ref=hbm.at[source],
                dst_ref=buf.at[landing],
                send_sem=z_send.at[which, step],
                recv_sem=z_recv.at[which, step],
                device_id=z_peer,
                device_id_type=MESH,
            )
            for which, (hbm, buf) in enumerate(((k_hbm, zk), (v_hbm, zv)))
        ]

    def c_copies(sender):
        landing = pl.ds(pl.multiple_of(2 * rows * sender, rows), rows)
        return [
            pltpu.make_async_remote_copy(
                src_ref=hbm,
                dst_ref=buf.at[landing],
                send_sem=c_send.at[which],
                recv_sem=c_recv.at[which],
                device_id=chip_peer,
                device_id_type=MESH,
            )
            for which, (hbm, buf) in enumerate(((k_hbm, kbuf), (v_hbm, vbuf)))
        ]

    def a_copy(step, core):
        here = pl.ds(pl.multiple_of(2 * R * step + R * core, R), R)
        return pltpu.make_async_remote_copy(
            src_ref=attended.at[here],
            dst_ref=attended.at[here],
            send_sem=a_send.at[step],
            recv_sem=a_recv.at[step],
            device_id=chip_peer,
            device_id_type=MESH,
        )

    def o_copy(step):
        return pltpu.make_async_remote_copy(
            src_ref=terms.at[pl.ds(pl.multiple_of(2 * R * step + R * (1 - sub), R), R)],
            dst_ref=own_in.at[pl.ds(pl.multiple_of(R * step, R), R)],
            send_sem=o_send.at[step],
            recv_sem=o_recv.at[step],
            device_id=chip_peer,
            device_id_type=MESH,
        )

    def x_copy(step, part, core):
        at = pl.ds(part * cols, cols)
        return pltpu.make_async_remote_copy(
            src_ref=terms.at[pl.ds(pl.multiple_of(2 * R * step + R * core, R), R), at],
            dst_ref=x_in.at[pl.ds(pl.multiple_of(R * step, R), R), at],
            send_sem=x_send.at[step, part, core],
            recv_sem=x_recv.at[step, part],
            device_id={"heads": 1 - group, "sub": core},
            device_id_type=MESH,
        )

    @pl.when(has_z)
    def _():
        for step in range(steps):
            for copy in z_copies(step):
                copy.start()

    for copy in c_copies(sub):
        copy.start()

    kbuf[z_rows, :] = jnp.zeros((rows, width), kbuf.dtype)
    vbuf[z_rows, :] = jnp.zeros((rows, width), vbuf.dtype)

    def turn(block):
        source = pl.ds(pl.multiple_of(block * CHUNK, CHUNK), CHUNK)
        for head in range(heads_here):
            lanes = pl.ds(head * HD, HD)
            kt[block, lanes, :] = kbuf[source, lanes].T

    def turn_all(start):
        lax.fori_loop(0, rows // CHUNK, lambda i, c: (turn(start + i), c)[1], 0)

    def query_row(step):
        return pl.multiple_of(jnp.where(sub == 0, rows - R - step * R, step * R), R)

    locals_[0].wait()
    turn_all(rows // CHUNK)
    turn_all(2 * sub * rows // CHUNK)
    for copy in locals_[1:3]:
        copy.wait()
    for copy in c_copies(1 - sub):
        copy.wait_recv()
    turn_all(2 * (1 - sub) * rows // CHUNK)
    locals_[3].wait()

    def finish(step):
        for part in range(PARTS):
            x_copy(step, part, 0).wait_recv()
        here = pl.ds(pl.multiple_of(R * step, R), R)
        target = pl.ds(query_row(step), R)

        def add(own):
            out_ref[target, :] = (own.astype(jnp.float32) + x_in[here, :].astype(jnp.float32)).astype(
                out_ref.dtype
            )

        @pl.when(sends_x)
        def _():
            o_copy(step).wait_recv()
            add(own_in[here, :])

        @pl.when(jnp.logical_not(sends_x))
        def _():
            add(terms[pl.ds(pl.multiple_of(2 * R * step + R * sub, R), R), :])

    ones = jnp.ones((span, HD), jnp.bfloat16)

    def one_step(step, carry):
        row = query_row(step)
        queries_here = pl.ds(row, R)
        base_block = row // CHUNK
        base = pl.multiple_of(base_block * CHUNK, CHUNK)
        lead = row - base
        keys_here = pl.ds(base, span)

        @pl.when(has_z)
        def _():
            for copy in z_copies(step):
                copy.wait_recv()
            landed = pl.ds(pl.multiple_of(step * R, R), R)
            start = jnp.where(sub == 0, row, 2 * rows + row)
            place = pl.ds(pl.multiple_of(start, R), R)
            kbuf[place, :] = zk[landed, :]
            vbuf[place, :] = zv[landed, :]
            turn(start // CHUNK)

        row_at = lax.broadcasted_iota(jnp.int32, (R, span), 0)
        key_at = lax.broadcasted_iota(jnp.int32, (R, span), 1)
        key_pos = key_at + (first + base - rows)
        distance[...] = jnp.where(
            (key_pos >= 0) & (key_pos < length_end), jnp.abs(row_at + (rows + lead) - key_at), FAR
        )
        row_fine = (lax.broadcasted_iota(jnp.int32, (R, HD), 0) + (first + row)) < length_end
        done = pl.ds(pl.multiple_of(2 * R * step + R * sub, R), R)

        def score(head, slot):
            lanes = pl.ds(head * HD, HD)
            block_keys = jnp.concatenate(
                [kt[base_block + block, lanes, :] for block in range(blocks)], axis=1
            )
            raw = jnp.dot(qbuf[queries_here, lanes], block_keys, preferred_element_type=jnp.float32)
            raw = jnp.where(distance[...] <= half_width[group * heads_here + head], raw, CLOSED)
            scores[slot][...] = raw
            top = raw[:, :CHUNK]
            for block in range(1, blocks):
                top = jnp.maximum(top, raw[:, block * CHUNK : (block + 1) * CHUNK])
            tops[slot][...] = jnp.broadcast_to(jnp.max(top, axis=1, keepdims=True), (R, CHUNK))

        def weigh(slot):
            top = tops[slot][...]
            for block in range(blocks):
                at = pl.ds(block * CHUNK, CHUNK)
                weights[slot][:, at] = jnp.exp2((scores[slot][:, at] - top) * EXP2_SCALE).astype(
                    jnp.bfloat16
                )

        def gather(head, slot):
            lanes = pl.ds(head * HD, HD)
            values = jnp.concatenate([vbuf[keys_here, lanes], ones], axis=1)
            sums = jnp.dot(weights[slot][...], values, preferred_element_type=jnp.float32)
            attended[done, lanes] = jnp.where(row_fine, sums[:, :HD] / sums[:, HD:], 0.0).astype(
                attended.dtype
            )

        stages = heads_here // G
        for stage in range(stages + 2):
            for one in range(G):
                if stage < stages:
                    score(stage * G + one, stage % 2 * G + one)
                if 1 <= stage <= stages:
                    weigh((stage - 1) % 2 * G + one)
                if stage >= 2:
                    gather((stage - 2) * G + one, stage % 2 * G + one)

        a_copy(step, sub).start()
        a_copy(step, 1 - sub).wait_recv()
        both = pl.ds(pl.multiple_of(2 * R * step, 2 * R), 2 * R)
        for part in range(PARTS):
            at = pl.ds(part * cols, cols)
            terms[both, at] = jnp.dot(
                attended[both, :], wbuf[:, at], preferred_element_type=jnp.float32
            ).astype(terms.dtype)

            @pl.when(sends_x)
            def _():
                for core in range(2):
                    x_copy(step, part, core).start()

        @pl.when(jnp.logical_not(sends_x))
        def _():
            o_copy(step).start()

        @pl.when(step >= 2)
        def _():
            finish(step - 2)

        return carry

    lax.fori_loop(0, steps, one_step, 0)
    finish(steps - 2)
    finish(steps - 1)

    for copy in c_copies(sub):
        copy.wait_send()
    for step in range(steps):
        a_copy(step, sub).wait_send()

    @pl.when(sends_x)
    def _():
        for step in range(steps):
            for part in range(PARTS):
                for core in range(2):
                    x_copy(step, part, core).wait_send()

    @pl.when(jnp.logical_not(sends_x))
    def _():
        for step in range(steps):
            o_copy(step).wait_send()

    @pl.when(has_z)
    def _():
        for step in range(steps):
            for copy in z_copies(step):
                copy.wait_send()


def local(queries, keys, values, half_width, valid_length, out_weight):
    rows, width = queries.shape
    bf16, f32 = jnp.bfloat16, jnp.float32
    dma = pltpu.SemaphoreType.DMA
    steps = rows // R
    span = 2 * rows + CHUNK
    whole = pltpu.VMEM((rows, width), bf16)
    return pl.pallas_call(
        kernel,
        out_shape=pltpu.VMEM((rows, width), bf16),
        in_specs=[pl.BlockSpec(memory_space=pltpu.SMEM)] * 2
        + [pl.BlockSpec(memory_space=pl.ANY)] * 4,
        out_specs=pl.BlockSpec(memory_space=pltpu.VMEM),
        scratch_shapes=[
            whole,
            pltpu.VMEM((3 * rows, width), bf16),
            pltpu.VMEM((3 * rows, width), bf16),
            whole,
            whole,
            pltpu.VMEM((3 * rows // CHUNK, width, CHUNK), bf16),
            pltpu.VMEM(out_weight.shape, bf16),
            pltpu.VMEM((R, span), jnp.int32),
            pltpu.VMEM((2 * rows, width), bf16),
            pltpu.VMEM((2 * rows, width), bf16),
            whole,
            whole,
            [pltpu.VMEM((R, span), f32)] * (2 * G),
            [pltpu.VMEM((R, CHUNK), f32)] * (2 * G),
            [pltpu.VMEM((R, span), bf16)] * (2 * G),
            dma((4,)),
            dma((2, steps)),
            dma((2, steps)),
            dma((2,)),
            dma((2,)),
            dma((steps,)),
            dma((steps,)),
            dma((steps,)),
            dma((steps,)),
            dma((steps, PARTS, 2)),
            dma((steps, PARTS)),
        ],
        compiler_params=pltpu.CompilerParams(
            collective_id=0, has_side_effects=True, vmem_limit_bytes=56 << 20
        ),
    )(half_width, valid_length, queries, keys, values, out_weight)


def solution(mesh):
    placed = (
        P(("parts", "seq", "sub"), "heads"),
        P(("parts", "seq", "sub"), "heads"),
        P(("parts", "seq", "sub"), "heads"),
        P(),
        P("parts"),
        P("heads", "sub"),
    )
    return jax.shard_map(
        local,
        mesh=mesh,
        in_specs=placed,
        out_specs=P(("parts", "seq", "sub"), "heads"),
        check_vma=False,
    )
```

```python
import math

import jax
import jax.numpy as jnp
from jax import lax
from jax.experimental import pallas as pl
from jax.experimental.pallas import tpu as pltpu
from jax.sharding import PartitionSpec as P

HD = 128
R = 64
CHUNK = 128
PARTS = 4
G = 2
CLOSED = -1e30
FAR = 1 << 20
EXP2_SCALE = math.log2(math.e) / math.sqrt(HD)
MESH = pl.DeviceIdType.MESH


def kernel(
    half_width,
    valid_length,
    q_hbm,
    k_hbm,
    v_hbm,
    w_hbm,
    out_ref,
    qbuf,
    kbuf,
    vbuf,
    zk,
    zv,
    kt,
    wbuf,
    distance,
    attended,
    terms,
    own_in,
    x_in,
    scores,
    tops,
    totals,
    weights,
    partial,
    local_sem,
    z_send,
    z_recv,
    c_send,
    c_recv,
    a_send,
    a_recv,
    o_send,
    o_recv,
    x_send,
    x_recv,
):
    rows, width = qbuf.shape
    heads_here = width // HD
    steps = rows // R
    blocks = 2 * rows // CHUNK + 1
    span = blocks * CHUNK
    cols = width // PARTS
    split = width * 3 // 4
    seq = lax.axis_index("seq")
    group = lax.axis_index("heads")
    sub = lax.axis_index("sub")
    has_z = jnp.where(sub == 0, seq > 0, seq < lax.axis_size("seq") - 1)
    sends_x = sub == 1 - group
    chip_peer = {"sub": 1 - sub}
    z_peer = {"seq": seq + 2 * sub - 1, "sub": 1 - sub}
    first = (seq * 2 + sub) * rows
    length_end = valid_length[0]

    barrier = pltpu.get_barrier_semaphore()
    pl.semaphore_signal(barrier, inc=1, device_id=chip_peer, device_id_type=MESH)
    for core in range(2):
        pl.semaphore_signal(
            barrier, inc=1, device_id={"heads": 1 - group, "sub": core}, device_id_type=MESH
        )

    @pl.when(has_z)
    def _():
        pl.semaphore_signal(barrier, inc=1, device_id=z_peer, device_id_type=MESH)

    own_rows = pl.ds(rows, rows)
    z_rows = pl.ds(pl.multiple_of(2 * rows * sub, rows), rows)
    locals_ = [
        pltpu.make_async_copy(k_hbm, kbuf.at[own_rows], local_sem.at[0]),
        pltpu.make_async_copy(q_hbm, qbuf, local_sem.at[1]),
        pltpu.make_async_copy(v_hbm, vbuf.at[own_rows], local_sem.at[2]),
        pltpu.make_async_copy(w_hbm, wbuf, local_sem.at[3]),
    ]
    for copy in locals_[:3]:
        copy.start()
    kbuf[z_rows, :] = jnp.zeros((rows, width), kbuf.dtype)
    vbuf[z_rows, :] = jnp.zeros((rows, width), vbuf.dtype)
    pl.semaphore_wait(barrier, 3 + has_z.astype(jnp.int32))

    def z_copies(step):
        start = jnp.where(sub == 0, step * R, rows - R - step * R)
        source = pl.ds(pl.multiple_of(start, R), R)
        landing = pl.ds(pl.multiple_of(step * R, R), R)
        return [
            pltpu.make_async_remote_copy(
                src_ref=hbm.at[source],
                dst_ref=buf.at[landing],
                send_sem=z_send.at[which, step],
                recv_sem=z_recv.at[which, step],
                device_id=z_peer,
                device_id_type=MESH,
            )
            for which, (hbm, buf) in enumerate(((k_hbm, zk), (v_hbm, zv)))
        ]

    def c_copies(sender):
        landing = pl.ds(pl.multiple_of(2 * rows * sender, rows), rows)
        return [
            pltpu.make_async_remote_copy(
                src_ref=hbm,
                dst_ref=buf.at[landing],
                send_sem=c_send.at[which],
                recv_sem=c_recv.at[which],
                device_id=chip_peer,
                device_id_type=MESH,
            )
            for which, (hbm, buf) in enumerate(((k_hbm, kbuf), (v_hbm, vbuf)))
        ]

    def a_copy(step, core, half):
        here = (
            pl.ds(pl.multiple_of(2 * R * step + R * core, R), R),
            pl.ds(half * split, (width - split) if half else split),
        )
        return pltpu.make_async_remote_copy(
            src_ref=attended.at[here],
            dst_ref=attended.at[here],
            send_sem=a_send.at[step, half],
            recv_sem=a_recv.at[step, half],
            device_id=chip_peer,
            device_id_type=MESH,
        )

    def o_copy(step):
        return pltpu.make_async_remote_copy(
            src_ref=terms.at[pl.ds(pl.multiple_of(2 * R * step + R * (1 - sub), R), R)],
            dst_ref=own_in.at[pl.ds(pl.multiple_of(R * step, R), R)],
            send_sem=o_send.at[step],
            recv_sem=o_recv.at[step],
            device_id=chip_peer,
            device_id_type=MESH,
        )

    def x_copy(step, part, core):
        at = pl.ds(part * cols, cols)
        return pltpu.make_async_remote_copy(
            src_ref=terms.at[pl.ds(pl.multiple_of(2 * R * step + R * core, R), R), at],
            dst_ref=x_in.at[pl.ds(pl.multiple_of(R * step, R), R), at],
            send_sem=x_send.at[step, part, core],
            recv_sem=x_recv.at[step, part],
            device_id={"heads": 1 - group, "sub": core},
            device_id_type=MESH,
        )

    @pl.when(has_z)
    def _():
        for step in range(steps):
            for copy in z_copies(step):
                copy.start()

    for copy in c_copies(sub):
        copy.start()

    def turn(block):
        source = pl.ds(pl.multiple_of(block * CHUNK, CHUNK), CHUNK)
        for head in range(heads_here):
            lanes = pl.ds(head * HD, HD)
            kt[block, lanes, :] = kbuf[source, lanes].T

    def turn_all(start):
        lax.fori_loop(0, rows // CHUNK, lambda i, c: (turn(start + i), c)[1], 0)

    def query_row(step):
        return pl.multiple_of(jnp.where(sub == 0, rows - R - step * R, step * R), R)

    locals_[0].wait()
    turn_all(rows // CHUNK)
    turn_all(2 * sub * rows // CHUNK)
    for copy in locals_[1:3]:
        copy.wait()
    locals_[3].start()
    for copy in c_copies(1 - sub):
        copy.wait_recv()
    turn_all(2 * (1 - sub) * rows // CHUNK)

    def finish(step):
        for part in range(PARTS):
            x_copy(step, part, 0).wait_recv()
        here = pl.ds(pl.multiple_of(R * step, R), R)
        target = pl.ds(query_row(step), R)

        def add(own):
            out_ref[target, :] = (own.astype(jnp.float32) + x_in[here, :].astype(jnp.float32)).astype(
                out_ref.dtype
            )

        @pl.when(sends_x)
        def _():
            o_copy(step).wait_recv()
            add(own_in[here, :])

        @pl.when(jnp.logical_not(sends_x))
        def _():
            add(terms[pl.ds(pl.multiple_of(2 * R * step + R * sub, R), R), :])

    def one_step(step, carry):
        row = query_row(step)
        queries_here = pl.ds(row, R)
        base_block = row // CHUNK
        base = pl.multiple_of(base_block * CHUNK, CHUNK)
        lead = row - base
        keys_here = pl.ds(base, span)

        @pl.when(has_z)
        def _():
            for copy in z_copies(step):
                copy.wait_recv()
            landed = pl.ds(pl.multiple_of(step * R, R), R)
            start = jnp.where(sub == 0, row, 2 * rows + row)
            place = pl.ds(pl.multiple_of(start, R), R)
            kbuf[place, :] = zk[landed, :]
            vbuf[place, :] = zv[landed, :]
            turn(start // CHUNK)

        row_at = lax.broadcasted_iota(jnp.int32, (R, span), 0)
        key_at = lax.broadcasted_iota(jnp.int32, (R, span), 1)
        key_pos = key_at + (first + base - rows)
        distance[...] = jnp.where(
            (key_pos >= 0) & (key_pos < length_end), jnp.abs(row_at + (rows + lead) - key_at), FAR
        )
        row_fine = (lax.broadcasted_iota(jnp.int32, (R, HD), 0) + (first + row)) < length_end
        done = pl.ds(pl.multiple_of(2 * R * step + R * sub, R), R)

        def score(head, slot):
            lanes = pl.ds(head * HD, HD)
            block_keys = jnp.concatenate(
                [kt[base_block + block, lanes, :] for block in range(blocks)], axis=1
            )
            raw = jnp.dot(qbuf[queries_here, lanes], block_keys, preferred_element_type=jnp.float32)
            raw = jnp.where(distance[...] <= half_width[group * heads_here + head], raw, CLOSED)
            scores[slot][...] = raw
            top = raw[:, :CHUNK]
            for block in range(1, blocks):
                top = jnp.maximum(top, raw[:, block * CHUNK : (block + 1) * CHUNK])
            tops[slot][...] = jnp.broadcast_to(jnp.max(top, axis=1, keepdims=True), (R, CHUNK))

        def weigh(slot):
            top = tops[slot][...]
            total = jnp.zeros((R, CHUNK), jnp.float32)
            for block in range(blocks):
                at = pl.ds(block * CHUNK, CHUNK)
                exact = jnp.exp2((scores[slot][:, at] - top) * EXP2_SCALE)
                total = total + exact
                weights[slot][:, at] = exact.astype(jnp.bfloat16)
            totals[slot][...] = jnp.broadcast_to(jnp.sum(total, axis=1, keepdims=True), (R, HD))

        def gather(head, slot):
            lanes = pl.ds(head * HD, HD)
            sums = jnp.dot(
                weights[slot][...], vbuf[keys_here, lanes], preferred_element_type=jnp.float32
            )
            attended[done, lanes] = jnp.where(row_fine, sums / totals[slot][...], 0.0).astype(
                attended.dtype
            )

        stages = heads_here // G
        for stage in range(stages + 2):
            for one in range(G):
                if stage < stages:
                    score(stage * G + one, stage % 2 * G + one)
                if 1 <= stage <= stages:
                    weigh((stage - 1) % 2 * G + one)
                if stage >= 2:
                    gather((stage - 2) * G + one, stage % 2 * G + one)
            if (stage - 1) * G * HD == split:
                a_copy(step, sub, 0).start()

        a_copy(step, sub, 1).start()
        a_copy(step, 1 - sub, 0).wait_recv()

        @pl.when(step == 0)
        def _():
            locals_[3].wait()

        both = pl.ds(pl.multiple_of(2 * R * step, 2 * R), 2 * R)
        early, late = (pl.ds(0, split), pl.ds(split, width - split))
        for part in range(PARTS):
            at = pl.ds(part * cols, cols)
            partial[:, at] = jnp.dot(
                attended[both, early], wbuf[early, at], preferred_element_type=jnp.float32
            )
        a_copy(step, 1 - sub, 1).wait_recv()
        for part in range(PARTS):
            at = pl.ds(part * cols, cols)
            terms[both, at] = (
                partial[:, at]
                + jnp.dot(attended[both, late], wbuf[late, at], preferred_element_type=jnp.float32)
            ).astype(terms.dtype)

            @pl.when(sends_x)
            def _():
                for core in range(2):
                    x_copy(step, part, core).start()

        @pl.when(jnp.logical_not(sends_x))
        def _():
            o_copy(step).start()

        @pl.when(step >= 2)
        def _():
            finish(step - 2)

        return carry

    lax.fori_loop(0, steps, one_step, 0)
    finish(steps - 2)
    finish(steps - 1)

    for copy in c_copies(sub):
        copy.wait_send()
    for step in range(steps):
        for half in range(2):
            a_copy(step, sub, half).wait_send()

    @pl.when(sends_x)
    def _():
        for step in range(steps):
            for part in range(PARTS):
                for core in range(2):
                    x_copy(step, part, core).wait_send()

    @pl.when(jnp.logical_not(sends_x))
    def _():
        for step in range(steps):
            o_copy(step).wait_send()

    @pl.when(has_z)
    def _():
        for step in range(steps):
            for copy in z_copies(step):
                copy.wait_send()


def local(queries, keys, values, half_width, valid_length, out_weight):
    rows, width = queries.shape
    bf16, f32 = jnp.bfloat16, jnp.float32
    dma = pltpu.SemaphoreType.DMA
    steps = rows // R
    span = 2 * rows + CHUNK
    whole = pltpu.VMEM((rows, width), bf16)
    return pl.pallas_call(
        kernel,
        out_shape=pltpu.VMEM((rows, width), bf16),
        in_specs=[pl.BlockSpec(memory_space=pltpu.SMEM)] * 2
        + [pl.BlockSpec(memory_space=pl.ANY)] * 4,
        out_specs=pl.BlockSpec(memory_space=pltpu.VMEM),
        scratch_shapes=[
            whole,
            pltpu.VMEM((3 * rows, width), bf16),
            pltpu.VMEM((3 * rows, width), bf16),
            whole,
            whole,
            pltpu.VMEM((3 * rows // CHUNK, width, CHUNK), bf16),
            pltpu.VMEM(out_weight.shape, bf16),
            pltpu.VMEM((R, span), jnp.int32),
            pltpu.VMEM((2 * rows, width), bf16),
            pltpu.VMEM((2 * rows, width), bf16),
            whole,
            whole,
            [pltpu.VMEM((R, span), f32)] * (2 * G),
            [pltpu.VMEM((R, CHUNK), f32)] * (2 * G),
            [pltpu.VMEM((R, HD), f32)] * (2 * G),
            [pltpu.VMEM((R, span), bf16)] * (2 * G),
            pltpu.VMEM((2 * R, width), f32),
            dma((4,)),
            dma((2, steps)),
            dma((2, steps)),
            dma((2,)),
            dma((2,)),
            dma((steps, 2)),
            dma((steps, 2)),
            dma((steps,)),
            dma((steps,)),
            dma((steps, PARTS, 2)),
            dma((steps, PARTS)),
        ],
        compiler_params=pltpu.CompilerParams(
            collective_id=0, has_side_effects=True, vmem_limit_bytes=56 << 20
        ),
    )(half_width, valid_length, queries, keys, values, out_weight)


def solution(mesh):
    placed = (
        P(("parts", "seq", "sub"), "heads"),
        P(("parts", "seq", "sub"), "heads"),
        P(("parts", "seq", "sub"), "heads"),
        P(),
        P("parts"),
        P("heads", "sub"),
    )
    return jax.shard_map(
        local,
        mesh=mesh,
        in_specs=placed,
        out_specs=P(("parts", "seq", "sub"), "heads"),
        check_vma=False,
    )
```

```python
import math

import jax
import jax.numpy as jnp
from jax import lax
from jax.experimental import pallas as pl
from jax.experimental.pallas import tpu as pltpu
from jax.sharding import PartitionSpec as P

HD = 128
R = 64
CHUNK = 128
PARTS = 4
G = 2
GROUPS = 4
CLOSED = -1e30
FAR = 1 << 20
EXP2_SCALE = math.log2(math.e) / math.sqrt(HD)
MESH = pl.DeviceIdType.MESH


def kernel(
    half_width,
    valid_length,
    q_hbm,
    k_hbm,
    v_hbm,
    w_hbm,
    out_ref,
    qbuf,
    kbuf,
    vbuf,
    zk,
    zv,
    kt,
    wbuf,
    distance,
    near_distance,
    near_sums,
    near_tops,
    near_totals,
    near_scores,
    near_weights,
    attended,
    terms,
    own_in,
    x_in,
    scores,
    tops,
    totals,
    fixes,
    weights,
    partial,
    local_sem,
    z_send,
    z_recv,
    c_send,
    c_recv,
    a_send,
    a_recv,
    o_send,
    o_recv,
    x_send,
    x_recv,
):
    rows, width = qbuf.shape
    heads_here = width // HD
    steps = rows // R
    own_blocks = rows // CHUNK
    pairs = rows // CHUNK
    lot = width // GROUPS
    cols = width // PARTS
    split = width * 3 // 4
    seq = lax.axis_index("seq")
    group = lax.axis_index("heads")
    sub = lax.axis_index("sub")
    has_z = jnp.where(sub == 0, seq > 0, seq < lax.axis_size("seq") - 1)
    sends_x = sub == 1 - group
    chip_peer = {"sub": 1 - sub}
    z_peer = {"seq": seq + 2 * sub - 1, "sub": 1 - sub}
    first = (seq * 2 + sub) * rows
    length_end = valid_length[0]

    barrier = pltpu.get_barrier_semaphore()
    pl.semaphore_signal(barrier, inc=1, device_id=chip_peer, device_id_type=MESH)
    for core in range(2):
        pl.semaphore_signal(
            barrier, inc=1, device_id={"heads": 1 - group, "sub": core}, device_id_type=MESH
        )

    @pl.when(has_z)
    def _():
        pl.semaphore_signal(barrier, inc=1, device_id=z_peer, device_id_type=MESH)

    own_rows = pl.ds(rows, rows)
    z_rows = pl.ds(pl.multiple_of(2 * rows * sub, rows), rows)
    locals_ = [
        pltpu.make_async_copy(k_hbm, kbuf.at[own_rows], local_sem.at[0]),
        pltpu.make_async_copy(q_hbm, qbuf, local_sem.at[1]),
        pltpu.make_async_copy(v_hbm, vbuf.at[own_rows], local_sem.at[2]),
        pltpu.make_async_copy(w_hbm, wbuf, local_sem.at[3]),
    ]
    for copy in locals_[:3]:
        copy.start()
    kbuf[z_rows, :] = jnp.zeros((rows, width), kbuf.dtype)
    vbuf[z_rows, :] = jnp.zeros((rows, width), vbuf.dtype)
    pl.semaphore_wait(barrier, 3 + has_z.astype(jnp.int32))

    def z_copies(step):
        start = jnp.where(sub == 0, step * R, rows - R - step * R)
        source = pl.ds(pl.multiple_of(start, R), R)
        landing = pl.ds(pl.multiple_of(step * R, R), R)
        return [
            pltpu.make_async_remote_copy(
                src_ref=hbm.at[source],
                dst_ref=buf.at[landing],
                send_sem=z_send.at[which, step],
                recv_sem=z_recv.at[which, step],
                device_id=z_peer,
                device_id_type=MESH,
            )
            for which, (hbm, buf) in enumerate(((k_hbm, zk), (v_hbm, zv)))
        ]

    def c_copies(sender, part):
        at = pl.ds(pl.multiple_of(part * lot, lot), lot)
        landing = (pl.ds(pl.multiple_of(2 * rows * sender, rows), rows), at)
        return [
            pltpu.make_async_remote_copy(
                src_ref=hbm.at[:, at],
                dst_ref=buf.at[landing],
                send_sem=c_send.at[which, part],
                recv_sem=c_recv.at[which, part],
                device_id=chip_peer,
                device_id_type=MESH,
            )
            for which, (hbm, buf) in enumerate(((k_hbm, kbuf), (v_hbm, vbuf)))
        ]

    def a_copy(step, core, half):
        here = (
            pl.ds(pl.multiple_of(2 * R * step + R * core, R), R),
            pl.ds(half * split, (width - split) if half else split),
        )
        return pltpu.make_async_remote_copy(
            src_ref=attended.at[here],
            dst_ref=attended.at[here],
            send_sem=a_send.at[step, half],
            recv_sem=a_recv.at[step, half],
            device_id=chip_peer,
            device_id_type=MESH,
        )

    def o_copy(step):
        return pltpu.make_async_remote_copy(
            src_ref=terms.at[pl.ds(pl.multiple_of(2 * R * step + R * (1 - sub), R), R)],
            dst_ref=own_in.at[pl.ds(pl.multiple_of(R * step, R), R)],
            send_sem=o_send.at[step],
            recv_sem=o_recv.at[step],
            device_id=chip_peer,
            device_id_type=MESH,
        )

    def x_copy(step, part, core):
        at = pl.ds(part * cols, cols)
        return pltpu.make_async_remote_copy(
            src_ref=terms.at[pl.ds(pl.multiple_of(2 * R * step + R * core, R), R), at],
            dst_ref=x_in.at[pl.ds(pl.multiple_of(R * step, R), R), at],
            send_sem=x_send.at[step, part, core],
            recv_sem=x_recv.at[step, part],
            device_id={"heads": 1 - group, "sub": core},
            device_id_type=MESH,
        )

    def send_z(begin, end):
        @pl.when(has_z)
        def _():
            for step in range(begin, end):
                for copy in z_copies(step):
                    copy.start()

    send_z(0, 1)
    for part in range(GROUPS):
        for copy in c_copies(sub, part):
            copy.start()
    send_z(1, steps)

    def turn(block, head):
        source = pl.ds(pl.multiple_of(block * CHUNK, CHUNK), CHUNK)
        lanes = pl.ds(pl.multiple_of(head * HD, HD), HD)
        kt[block, lanes, :] = kbuf[source, lanes].T

    def query_row(step):
        return pl.multiple_of(jnp.where(sub == 0, rows - R - step * R, step * R), R)

    locals_[0].wait()

    def turn_own(head, carry):
        for block in range(own_blocks):
            turn(own_blocks + block, head)
        return carry

    lax.fori_loop(0, heads_here, turn_own, 0)
    for copy in locals_[1:3]:
        copy.wait()
    locals_[3].start()

    def finish(step):
        for part in range(PARTS):
            x_copy(step, part, 0).wait_recv()
        here = pl.ds(pl.multiple_of(R * step, R), R)
        target = pl.ds(query_row(step), R)

        def add(own):
            out_ref[target, :] = (own.astype(jnp.float32) + x_in[here, :].astype(jnp.float32)).astype(
                out_ref.dtype
            )

        @pl.when(sends_x)
        def _():
            o_copy(step).wait_recv()
            add(own_in[here, :])

        @pl.when(jnp.logical_not(sends_x))
        def _():
            add(terms[pl.ds(pl.multiple_of(2 * R * step + R * sub, R), R), :])

    def near_place(pair):
        row = pl.multiple_of(jnp.where(sub == 0, rows - CHUNK - pair * CHUNK, pair * CHUNK), CHUNK)
        return row, jnp.where(sub == 0, own_blocks, pair)

    def keys_fine(key_pos):
        return (key_pos >= 0) & (key_pos < length_end)

    def near_masks(pair):
        row, block = near_place(pair)
        span = (2 * own_blocks - pair) * CHUNK
        row_at = lax.broadcasted_iota(jnp.int32, (CHUNK, span), 0) + (rows + row)
        key_at = lax.broadcasted_iota(jnp.int32, (CHUNK, span), 1) + block * CHUNK
        near_distance[:, :span] = jnp.where(
            keys_fine(key_at + (first - rows)), jnp.abs(row_at - key_at), FAR
        )

    def near_group(pair, part):
        row, first_block = near_place(pair)
        blocks = 2 * own_blocks - pair
        span = blocks * CHUNK
        keys_here = pl.ds(pl.multiple_of(first_block * CHUNK, CHUNK), span)
        queries_here = pl.ds(row, CHUNK)
        side = pair % 2
        count = heads_here // GROUPS
        lanes_of = [
            pl.ds(pl.multiple_of((part * count + one) * HD, HD), HD) for one in range(count)
        ]
        for one, lanes in enumerate(lanes_of):
            block_keys = jnp.concatenate(
                [kt[first_block + block, lanes, :] for block in range(blocks)], axis=1
            )
            raw = jnp.dot(qbuf[queries_here, lanes], block_keys, preferred_element_type=jnp.float32)
            wide = half_width[group * heads_here + part * count + one]
            raw = jnp.where(near_distance[:, :span] <= wide, raw, CLOSED)
            near_scores[one][:, :span] = raw
            top = raw[:, :CHUNK]
            for block in range(1, blocks):
                top = jnp.maximum(top, raw[:, block * CHUNK : (block + 1) * CHUNK])
            near_tops[side][:, lanes] = jnp.broadcast_to(
                jnp.max(top, axis=1, keepdims=True), (CHUNK, HD)
            )
        for one, lanes in enumerate(lanes_of):
            top = near_tops[side][:, lanes]
            total = jnp.zeros((CHUNK, HD), jnp.float32)
            for block in range(blocks):
                at = pl.ds(block * CHUNK, CHUNK)
                exact = jnp.exp2((near_scores[one][:, at] - top) * EXP2_SCALE)
                total = total + exact
                near_weights[one][:, at] = exact.astype(jnp.bfloat16)
            near_totals[side][:, lanes] = jnp.broadcast_to(
                jnp.sum(total, axis=1, keepdims=True), (CHUNK, HD)
            )
        for one, lanes in enumerate(lanes_of):
            near_sums[side][:, lanes] = jnp.dot(
                near_weights[one][:, :span],
                vbuf[keys_here, lanes],
                preferred_element_type=jnp.float32,
            )

    def first_group(part, carry):
        for copy in c_copies(1 - sub, part):
            copy.wait_recv()
        count = heads_here // GROUPS
        for one in range(count):
            for block in range(own_blocks):
                turn(2 * own_blocks * (1 - sub) + block, part * count + one)
        near_group(0, part)
        return carry

    def near_groups(pair, begin, count):
        lax.fori_loop(0, count, lambda i, c: (near_group(pair, begin + i), c)[1], 0)

    def far_step(pair, step):
        row = query_row(step)
        queries_here = pl.ds(row, R)
        first_block = jnp.where(sub == 0, own_blocks - 1 - pair, 2 * own_blocks)
        blocks = pair + 1
        span = blocks * CHUNK
        keys_here = pl.ds(pl.multiple_of(first_block * CHUNK, CHUNK), span)
        side = pair % 2
        half = step % 2
        near_rows = pl.ds(pl.multiple_of(R * jnp.where(sub == 0, 1 - half, half), R), R)

        row_at = lax.broadcasted_iota(jnp.int32, (R, span), 0) + (rows + row)
        key_at = lax.broadcasted_iota(jnp.int32, (R, span), 1) + first_block * CHUNK
        distance[:, :span] = jnp.where(
            keys_fine(key_at + (first - rows)), jnp.abs(row_at - key_at), FAR
        )
        row_fine = (lax.broadcasted_iota(jnp.int32, (R, HD), 0) + (first + row)) < length_end
        done = pl.ds(pl.multiple_of(2 * R * step + R * sub, R), R)

        @pl.when(has_z)
        def _():
            for copy in z_copies(step):
                copy.wait_recv()
            landed = pl.ds(pl.multiple_of(step * R, R), R)
            start = jnp.where(sub == 0, row, 2 * rows + row)
            place = pl.ds(pl.multiple_of(start, R), R)
            kbuf[place, :] = zk[landed, :]
            vbuf[place, :] = zv[landed, :]
            for head in range(heads_here):
                turn(start // CHUNK, head)

        def score(head, slot):
            lanes = pl.ds(head * HD, HD)
            block_keys = jnp.concatenate(
                [kt[first_block + block, lanes, :] for block in range(blocks)], axis=1
            )
            raw = jnp.dot(qbuf[queries_here, lanes], block_keys, preferred_element_type=jnp.float32)
            wide = half_width[group * heads_here + head]
            raw = jnp.where(distance[:, :span] <= wide, raw, CLOSED)
            scores[slot][:, :span] = raw
            top = raw[:, :CHUNK]
            for block in range(1, blocks):
                top = jnp.maximum(top, raw[:, block * CHUNK : (block + 1) * CHUNK])
            top = jnp.broadcast_to(jnp.max(top, axis=1, keepdims=True), (R, HD))
            tops[slot][...] = jnp.maximum(top, near_tops[side][near_rows, lanes])

        def weigh(head, slot):
            lanes = pl.ds(head * HD, HD)
            top = tops[slot][...]
            fixes[slot][...] = jnp.exp2((near_tops[side][near_rows, lanes] - top) * EXP2_SCALE)
            total = jnp.zeros((R, CHUNK), jnp.float32)
            for block in range(blocks):
                at = pl.ds(block * CHUNK, CHUNK)
                exact = jnp.exp2((scores[slot][:, at] - top) * EXP2_SCALE)
                total = total + exact
                weights[slot][:, at] = exact.astype(jnp.bfloat16)
            totals[slot][...] = jnp.broadcast_to(jnp.sum(total, axis=1, keepdims=True), (R, HD))

        def gather(head, slot):
            lanes = pl.ds(head * HD, HD)
            fix = fixes[slot][...]
            sums = near_sums[side][near_rows, lanes] * fix + jnp.dot(
                weights[slot][:, :span], vbuf[keys_here, lanes], preferred_element_type=jnp.float32
            )
            total = near_totals[side][near_rows, lanes] * fix + totals[slot][...]
            attended[done, lanes] = jnp.where(row_fine, sums / total, 0.0).astype(attended.dtype)

        stages = heads_here // G
        for stage in range(stages + 2):
            for one in range(G):
                if stage < stages:
                    score(stage * G + one, stage % 2 * G + one)
                if 1 <= stage <= stages:
                    weigh((stage - 1) * G + one, (stage - 1) % 2 * G + one)
                if stage >= 2:
                    gather((stage - 2) * G + one, stage % 2 * G + one)
            if (stage - 1) * G * HD == split:
                a_copy(step, sub, 0).start()
        a_copy(step, sub, 1).start()

    early, late = (pl.ds(0, split), pl.ds(split, width - split))

    def project_early(step):
        both = pl.ds(pl.multiple_of(2 * R * step, 2 * R), 2 * R)
        a_copy(step, 1 - sub, 0).wait_recv()
        for part in range(PARTS):
            at = pl.ds(part * cols, cols)
            partial[:, at] = jnp.dot(
                attended[both, early], wbuf[early, at], preferred_element_type=jnp.float32
            )
        a_copy(step, 1 - sub, 1).wait_recv()

    def project(step, begun):
        both = pl.ds(pl.multiple_of(2 * R * step, 2 * R), 2 * R)
        if begun:
            project_early(step)
        else:
            for half in range(2):
                a_copy(step, 1 - sub, half).wait_recv()
        for part in range(PARTS):
            at = pl.ds(part * cols, cols)
            if begun:
                shares = partial[:, at] + jnp.dot(
                    attended[both, late], wbuf[late, at], preferred_element_type=jnp.float32
                )
            else:
                shares = jnp.dot(attended[both, :], wbuf[:, at], preferred_element_type=jnp.float32)
            terms[both, at] = shares.astype(terms.dtype)

            @pl.when(sends_x)
            def _():
                for core in range(2):
                    x_copy(step, part, core).start()

        @pl.when(jnp.logical_not(sends_x))
        def _():
            o_copy(step).start()

    near_masks(0)
    lax.fori_loop(0, GROUPS, first_group, 0)
    far_step(0, 0)
    locals_[3].wait()
    project(0, True)
    near_masks(1)
    near_groups(1, 0, GROUPS // 2)
    far_step(0, 1)
    near_groups(1, GROUPS // 2, GROUPS // 2)
    project(1, False)

    for pair in range(1, pairs):
        more = pair + 1 < pairs
        if more:
            near_masks(pair + 1)

        def in_pair(half, carry):
            step = 2 * pair + half
            far_step(pair, step)
            if more:
                near_groups(pair + 1, half * (GROUPS // 2), GROUPS // 2)
            project(step, not more)
            finish(step - 2)
            return carry

        lax.fori_loop(0, 2, in_pair, 0)
    finish(steps - 2)
    finish(steps - 1)

    for part in range(GROUPS):
        for copy in c_copies(sub, part):
            copy.wait_send()
    for step in range(steps):
        for half in range(2):
            a_copy(step, sub, half).wait_send()

    @pl.when(sends_x)
    def _():
        for step in range(steps):
            for part in range(PARTS):
                for core in range(2):
                    x_copy(step, part, core).wait_send()

    @pl.when(jnp.logical_not(sends_x))
    def _():
        for step in range(steps):
            o_copy(step).wait_send()

    @pl.when(has_z)
    def _():
        for step in range(steps):
            for copy in z_copies(step):
                copy.wait_send()


def local(queries, keys, values, half_width, valid_length, out_weight):
    rows, width = queries.shape
    bf16, f32 = jnp.bfloat16, jnp.float32
    dma = pltpu.SemaphoreType.DMA
    steps = rows // R
    near = 2 * rows
    count = width // HD // GROUPS
    whole = pltpu.VMEM((rows, width), bf16)
    return pl.pallas_call(
        kernel,
        out_shape=pltpu.VMEM((rows, width), bf16),
        in_specs=[pl.BlockSpec(memory_space=pltpu.SMEM)] * 2
        + [pl.BlockSpec(memory_space=pl.ANY)] * 4,
        out_specs=pl.BlockSpec(memory_space=pltpu.VMEM),
        scratch_shapes=[
            whole,
            pltpu.VMEM((3 * rows, width), bf16),
            pltpu.VMEM((3 * rows, width), bf16),
            whole,
            whole,
            pltpu.VMEM((3 * rows // CHUNK, width, CHUNK), bf16),
            pltpu.VMEM(out_weight.shape, bf16),
            pltpu.VMEM((R, rows), jnp.int32),
            pltpu.VMEM((CHUNK, near), jnp.int32),
            [pltpu.VMEM((CHUNK, width), f32)] * 2,
            [pltpu.VMEM((CHUNK, width), f32)] * 2,
            [pltpu.VMEM((CHUNK, width), f32)] * 2,
            [pltpu.VMEM((CHUNK, near), f32)] * count,
            [pltpu.VMEM((CHUNK, near), bf16)] * count,
            pltpu.VMEM((2 * rows, width), bf16),
            pltpu.VMEM((2 * rows, width), bf16),
            whole,
            whole,
            [pltpu.VMEM((R, rows), f32)] * (2 * G),
            [pltpu.VMEM((R, CHUNK), f32)] * (2 * G),
            [pltpu.VMEM((R, HD), f32)] * (2 * G),
            [pltpu.VMEM((R, HD), f32)] * (2 * G),
            [pltpu.VMEM((R, rows), bf16)] * (2 * G),
            pltpu.VMEM((2 * R, width), f32),
            dma((4,)),
            dma((2, steps)),
            dma((2, steps)),
            dma((2, GROUPS)),
            dma((2, GROUPS)),
            dma((steps, 2)),
            dma((steps, 2)),
            dma((steps,)),
            dma((steps,)),
            dma((steps, PARTS, 2)),
            dma((steps, PARTS)),
        ],
        compiler_params=pltpu.CompilerParams(
            collective_id=0, has_side_effects=True, vmem_limit_bytes=60 << 20
        ),
    )(half_width, valid_length, queries, keys, values, out_weight)


def solution(mesh):
    placed = (
        P(("parts", "seq", "sub"), "heads"),
        P(("parts", "seq", "sub"), "heads"),
        P(("parts", "seq", "sub"), "heads"),
        P(),
        P("parts"),
        P("heads", "sub"),
    )
    return jax.shard_map(
        local,
        mesh=mesh,
        in_specs=placed,
        out_specs=P(("parts", "seq", "sub"), "heads"),
        check_vma=False,
    )
```

```python
import math

import jax
import jax.numpy as jnp
from jax import lax
from jax.experimental import pallas as pl
from jax.experimental.pallas import tpu as pltpu
from jax.sharding import PartitionSpec as P

HD = 128
R = 64
CHUNK = 128
PARTS = 2
G = 2
GROUPS = 4
CLOSED = -1e30
FAR = 1 << 20
EXP2_SCALE = math.log2(math.e) / math.sqrt(HD)
MESH = pl.DeviceIdType.MESH


def kernel(
    half_width,
    valid_length,
    q_hbm,
    k_hbm,
    v_hbm,
    w_hbm,
    out_ref,
    qbuf,
    kbuf,
    vbuf,
    zk,
    zv,
    kt,
    wbuf,
    distance,
    near_distance,
    near_sums,
    near_tops,
    near_totals,
    near_scores,
    near_weights,
    attended,
    terms,
    own_in,
    x_in,
    scores,
    tops,
    totals,
    fixes,
    weights,
    partial,
    local_sem,
    z_send,
    z_recv,
    c_send,
    c_recv,
    a_send,
    a_recv,
    o_send,
    o_recv,
    x_send,
    x_recv,
):
    rows, width = qbuf.shape
    heads_here = width // HD
    steps = rows // R
    own_blocks = rows // CHUNK
    pairs = rows // CHUNK
    lot = width // GROUPS
    cols = width // PARTS
    split = width * 3 // 4
    seq = lax.axis_index("seq")
    group = lax.axis_index("heads")
    sub = lax.axis_index("sub")
    has_z = jnp.where(sub == 0, seq > 0, seq < lax.axis_size("seq") - 1)
    sends_x = sub == 1 - group
    chip_peer = {"sub": 1 - sub}
    z_peer = {"seq": seq + 2 * sub - 1, "sub": 1 - sub}
    first = (seq * 2 + sub) * rows
    length_end = valid_length[0]

    barrier = pltpu.get_barrier_semaphore()
    pl.semaphore_signal(barrier, inc=1, device_id=chip_peer, device_id_type=MESH)
    for core in range(2):
        pl.semaphore_signal(
            barrier, inc=1, device_id={"heads": 1 - group, "sub": core}, device_id_type=MESH
        )

    @pl.when(has_z)
    def _():
        pl.semaphore_signal(barrier, inc=1, device_id=z_peer, device_id_type=MESH)

    own_rows = pl.ds(rows, rows)
    z_rows = pl.ds(pl.multiple_of(2 * rows * sub, rows), rows)
    locals_ = [
        pltpu.make_async_copy(k_hbm, kbuf.at[own_rows], local_sem.at[0]),
        pltpu.make_async_copy(q_hbm, qbuf, local_sem.at[1]),
        pltpu.make_async_copy(v_hbm, vbuf.at[own_rows], local_sem.at[2]),
        pltpu.make_async_copy(w_hbm, wbuf, local_sem.at[3]),
    ]
    for copy in locals_[:3]:
        copy.start()
    kbuf[z_rows, :] = jnp.zeros((rows, width), kbuf.dtype)
    vbuf[z_rows, :] = jnp.zeros((rows, width), vbuf.dtype)
    pl.semaphore_wait(barrier, 3 + has_z.astype(jnp.int32))

    def z_copies(step):
        start = jnp.where(sub == 0, step * R, rows - R - step * R)
        source = pl.ds(pl.multiple_of(start, R), R)
        landing = pl.ds(pl.multiple_of(step * R, R), R)
        return [
            pltpu.make_async_remote_copy(
                src_ref=hbm.at[source],
                dst_ref=buf.at[landing],
                send_sem=z_send.at[which, step],
                recv_sem=z_recv.at[which, step],
                device_id=z_peer,
                device_id_type=MESH,
            )
            for which, (hbm, buf) in enumerate(((k_hbm, zk), (v_hbm, zv)))
        ]

    def c_copies(sender, part):
        at = pl.ds(pl.multiple_of(part * lot, lot), lot)
        landing = (pl.ds(pl.multiple_of(2 * rows * sender, rows), rows), at)
        return [
            pltpu.make_async_remote_copy(
                src_ref=hbm.at[:, at],
                dst_ref=buf.at[landing],
                send_sem=c_send.at[which, part],
                recv_sem=c_recv.at[which, part],
                device_id=chip_peer,
                device_id_type=MESH,
            )
            for which, (hbm, buf) in enumerate(((k_hbm, kbuf), (v_hbm, vbuf)))
        ]

    def a_copy(step, core, half):
        here = (
            pl.ds(pl.multiple_of(2 * R * step + R * core, R), R),
            pl.ds(half * split, (width - split) if half else split),
        )
        return pltpu.make_async_remote_copy(
            src_ref=attended.at[here],
            dst_ref=attended.at[here],
            send_sem=a_send.at[step, half],
            recv_sem=a_recv.at[step, half],
            device_id=chip_peer,
            device_id_type=MESH,
        )

    def o_copy(step):
        return pltpu.make_async_remote_copy(
            src_ref=terms.at[pl.ds(pl.multiple_of(2 * R * step + R * (1 - sub), R), R)],
            dst_ref=own_in.at[pl.ds(pl.multiple_of(R * step, R), R)],
            send_sem=o_send.at[step],
            recv_sem=o_recv.at[step],
            device_id=chip_peer,
            device_id_type=MESH,
        )

    def x_copy(step, part, core):
        at = pl.ds(part * cols, cols)
        return pltpu.make_async_remote_copy(
            src_ref=terms.at[pl.ds(pl.multiple_of(2 * R * step + R * core, R), R), at],
            dst_ref=x_in.at[pl.ds(pl.multiple_of(R * step, R), R), at],
            send_sem=x_send.at[step, part, core],
            recv_sem=x_recv.at[step, part],
            device_id={"heads": 1 - group, "sub": core},
            device_id_type=MESH,
        )

    def send_z(begin, end):
        @pl.when(has_z)
        def _():
            for step in range(begin, end):
                for copy in z_copies(step):
                    copy.start()

    send_z(0, 1)
    for part in range(GROUPS):
        for copy in c_copies(sub, part):
            copy.start()
    send_z(1, steps)

    def turn(block, head):
        source = pl.ds(pl.multiple_of(block * CHUNK, CHUNK), CHUNK)
        lanes = pl.ds(pl.multiple_of(head * HD, HD), HD)
        kt[block, lanes, :] = kbuf[source, lanes].T

    def query_row(step):
        return pl.multiple_of(jnp.where(sub == 0, rows - R - step * R, step * R), R)

    locals_[0].wait()

    def turn_own(head, carry):
        for block in range(own_blocks):
            turn(own_blocks + block, head)
        return carry

    lax.fori_loop(0, heads_here, turn_own, 0)
    for copy in locals_[1:3]:
        copy.wait()
    locals_[3].start()

    def finish(step):
        for part in range(PARTS):
            x_copy(step, part, 0).wait_recv()
        here = pl.ds(pl.multiple_of(R * step, R), R)
        target = pl.ds(query_row(step), R)

        def add(own):
            out_ref[target, :] = (own.astype(jnp.float32) + x_in[here, :].astype(jnp.float32)).astype(
                out_ref.dtype
            )

        @pl.when(sends_x)
        def _():
            o_copy(step).wait_recv()
            add(own_in[here, :])

        @pl.when(jnp.logical_not(sends_x))
        def _():
            add(terms[pl.ds(pl.multiple_of(2 * R * step + R * sub, R), R), :])

    def near_place(pair):
        row = pl.multiple_of(jnp.where(sub == 0, rows - CHUNK - pair * CHUNK, pair * CHUNK), CHUNK)
        return row, jnp.where(sub == 0, own_blocks, pair)

    def keys_fine(key_pos):
        return (key_pos >= 0) & (key_pos < length_end)

    def near_masks(pair):
        row, block = near_place(pair)
        span = (2 * own_blocks - pair) * CHUNK
        row_at = lax.broadcasted_iota(jnp.int32, (CHUNK, span), 0) + (rows + row)
        key_at = lax.broadcasted_iota(jnp.int32, (CHUNK, span), 1) + block * CHUNK
        near_distance[:, :span] = jnp.where(
            keys_fine(key_at + (first - rows)), jnp.abs(row_at - key_at), FAR
        )

    def near_group(pair, part):
        row, first_block = near_place(pair)
        blocks = 2 * own_blocks - pair
        span = blocks * CHUNK
        keys_here = pl.ds(pl.multiple_of(first_block * CHUNK, CHUNK), span)
        queries_here = pl.ds(row, CHUNK)
        side = pair % 2
        count = heads_here // GROUPS
        lanes_of = [
            pl.ds(pl.multiple_of((part * count + one) * HD, HD), HD) for one in range(count)
        ]
        for one, lanes in enumerate(lanes_of):
            block_keys = jnp.concatenate(
                [kt[first_block + block, lanes, :] for block in range(blocks)], axis=1
            )
            raw = jnp.dot(qbuf[queries_here, lanes], block_keys, preferred_element_type=jnp.float32)
            wide = half_width[group * heads_here + part * count + one]
            raw = jnp.where(near_distance[:, :span] <= wide, raw, CLOSED)
            near_scores[one][:, :span] = raw
            top = raw[:, :CHUNK]
            for block in range(1, blocks):
                top = jnp.maximum(top, raw[:, block * CHUNK : (block + 1) * CHUNK])
            near_tops[side][:, lanes] = jnp.broadcast_to(
                jnp.max(top, axis=1, keepdims=True), (CHUNK, HD)
            )
        for one, lanes in enumerate(lanes_of):
            top = near_tops[side][:, lanes]
            total = jnp.zeros((CHUNK, HD), jnp.float32)
            for block in range(blocks):
                at = pl.ds(block * CHUNK, CHUNK)
                exact = jnp.exp2((near_scores[one][:, at] - top) * EXP2_SCALE)
                total = total + exact
                near_weights[one][:, at] = exact.astype(jnp.bfloat16)
            near_totals[side][:, lanes] = jnp.broadcast_to(
                jnp.sum(total, axis=1, keepdims=True), (CHUNK, HD)
            )
        for one, lanes in enumerate(lanes_of):
            near_sums[side][:, lanes] = jnp.dot(
                near_weights[one][:, :span],
                vbuf[keys_here, lanes],
                preferred_element_type=jnp.float32,
            )

    def first_group(part, carry):
        for copy in c_copies(1 - sub, part):
            copy.wait_recv()
        count = heads_here // GROUPS
        for one in range(count):
            for block in range(own_blocks):
                turn(2 * own_blocks * (1 - sub) + block, part * count + one)
        near_group(0, part)
        return carry

    def near_groups(pair, begin, count):
        lax.fori_loop(0, count, lambda i, c: (near_group(pair, begin + i), c)[1], 0)

    def far_step(pair, step):
        row = query_row(step)
        queries_here = pl.ds(row, R)
        first_block = jnp.where(sub == 0, own_blocks - 1 - pair, 2 * own_blocks)
        blocks = pair + 1
        span = blocks * CHUNK
        keys_here = pl.ds(pl.multiple_of(first_block * CHUNK, CHUNK), span)
        side = pair % 2
        half = step % 2
        near_rows = pl.ds(pl.multiple_of(R * jnp.where(sub == 0, 1 - half, half), R), R)

        row_at = lax.broadcasted_iota(jnp.int32, (R, span), 0) + (rows + row)
        key_at = lax.broadcasted_iota(jnp.int32, (R, span), 1) + first_block * CHUNK
        distance[:, :span] = jnp.where(
            keys_fine(key_at + (first - rows)), jnp.abs(row_at - key_at), FAR
        )
        row_fine = (lax.broadcasted_iota(jnp.int32, (R, HD), 0) + (first + row)) < length_end
        done = pl.ds(pl.multiple_of(2 * R * step + R * sub, R), R)

        @pl.when(has_z)
        def _():
            for copy in z_copies(step):
                copy.wait_recv()
            landed = pl.ds(pl.multiple_of(step * R, R), R)
            start = jnp.where(sub == 0, row, 2 * rows + row)
            place = pl.ds(pl.multiple_of(start, R), R)
            kbuf[place, :] = zk[landed, :]
            vbuf[place, :] = zv[landed, :]
            for head in range(heads_here):
                turn(start // CHUNK, head)

        def score(head, slot):
            lanes = pl.ds(head * HD, HD)
            block_keys = jnp.concatenate(
                [kt[first_block + block, lanes, :] for block in range(blocks)], axis=1
            )
            raw = jnp.dot(qbuf[queries_here, lanes], block_keys, preferred_element_type=jnp.float32)
            wide = half_width[group * heads_here + head]
            raw = jnp.where(distance[:, :span] <= wide, raw, CLOSED)
            scores[slot][:, :span] = raw
            top = raw[:, :CHUNK]
            for block in range(1, blocks):
                top = jnp.maximum(top, raw[:, block * CHUNK : (block + 1) * CHUNK])
            top = jnp.broadcast_to(jnp.max(top, axis=1, keepdims=True), (R, HD))
            tops[slot][...] = jnp.maximum(top, near_tops[side][near_rows, lanes])

        def weigh(head, slot):
            lanes = pl.ds(head * HD, HD)
            top = tops[slot][...]
            fixes[slot][...] = jnp.exp2((near_tops[side][near_rows, lanes] - top) * EXP2_SCALE)
            total = jnp.zeros((R, CHUNK), jnp.float32)
            for block in range(blocks):
                at = pl.ds(block * CHUNK, CHUNK)
                exact = jnp.exp2((scores[slot][:, at] - top) * EXP2_SCALE)
                total = total + exact
                weights[slot][:, at] = exact.astype(jnp.bfloat16)
            totals[slot][...] = jnp.broadcast_to(jnp.sum(total, axis=1, keepdims=True), (R, HD))

        def gather(head, slot):
            lanes = pl.ds(head * HD, HD)
            fix = fixes[slot][...]
            sums = near_sums[side][near_rows, lanes] * fix + jnp.dot(
                weights[slot][:, :span], vbuf[keys_here, lanes], preferred_element_type=jnp.float32
            )
            total = near_totals[side][near_rows, lanes] * fix + totals[slot][...]
            attended[done, lanes] = jnp.where(row_fine, sums / total, 0.0).astype(attended.dtype)

        stages = heads_here // G
        for stage in range(stages + 2):
            for one in range(G):
                if stage < stages:
                    score(stage * G + one, stage % 2 * G + one)
                if 1 <= stage <= stages:
                    weigh((stage - 1) * G + one, (stage - 1) % 2 * G + one)
                if stage >= 2:
                    gather((stage - 2) * G + one, stage % 2 * G + one)
            if (stage - 1) * G * HD == split:
                a_copy(step, sub, 0).start()
        a_copy(step, sub, 1).start()

    early, late = (pl.ds(0, split), pl.ds(split, width - split))

    def project_early(step):
        both = pl.ds(pl.multiple_of(2 * R * step, 2 * R), 2 * R)
        a_copy(step, 1 - sub, 0).wait_recv()
        for part in range(PARTS):
            at = pl.ds(part * cols, cols)
            partial[:, at] = jnp.dot(
                attended[both, early], wbuf[early, at], preferred_element_type=jnp.float32
            )
        a_copy(step, 1 - sub, 1).wait_recv()

    def project(step, begun):
        both = pl.ds(pl.multiple_of(2 * R * step, 2 * R), 2 * R)
        if begun:
            project_early(step)
        else:
            for half in range(2):
                a_copy(step, 1 - sub, half).wait_recv()
        for part in range(PARTS):
            at = pl.ds(part * cols, cols)
            if begun:
                shares = partial[:, at] + jnp.dot(
                    attended[both, late], wbuf[late, at], preferred_element_type=jnp.float32
                )
            else:
                shares = jnp.dot(attended[both, :], wbuf[:, at], preferred_element_type=jnp.float32)
            terms[both, at] = shares.astype(terms.dtype)

            @pl.when(sends_x)
            def _():
                for core in range(2):
                    x_copy(step, part, core).start()

        @pl.when(jnp.logical_not(sends_x))
        def _():
            o_copy(step).start()

    near_masks(0)
    lax.fori_loop(0, GROUPS, first_group, 0)
    far_step(0, 0)
    locals_[3].wait()
    project(0, True)
    near_masks(1)
    near_groups(1, 0, GROUPS // 2)
    far_step(0, 1)
    near_groups(1, GROUPS // 2, GROUPS // 2)
    project(1, False)

    for pair in range(1, pairs):
        more = pair + 1 < pairs
        if more:
            near_masks(pair + 1)

        def in_pair(half, carry):
            step = 2 * pair + half
            far_step(pair, step)
            if more:
                near_groups(pair + 1, half * (GROUPS // 2), GROUPS // 2)
            project(step, not more)
            finish(step - 2)
            return carry

        lax.fori_loop(0, 2, in_pair, 0)
    for part in range(GROUPS):
        for copy in c_copies(sub, part):
            copy.wait_send()
    for step in range(steps):
        for half in range(2):
            a_copy(step, sub, half).wait_send()

    @pl.when(has_z)
    def _():
        for step in range(steps):
            for copy in z_copies(step):
                copy.wait_send()

    def sent(begin, end):
        @pl.when(sends_x)
        def _():
            for step in range(begin, end):
                for part in range(PARTS):
                    for core in range(2):
                        x_copy(step, part, core).wait_send()

        @pl.when(jnp.logical_not(sends_x))
        def _():
            for step in range(begin, end):
                o_copy(step).wait_send()

    sent(0, steps - 2)
    finish(steps - 2)
    sent(steps - 2, steps - 1)
    finish(steps - 1)
    sent(steps - 1, steps)


def local(queries, keys, values, half_width, valid_length, out_weight):
    rows, width = queries.shape
    bf16, f32 = jnp.bfloat16, jnp.float32
    dma = pltpu.SemaphoreType.DMA
    steps = rows // R
    near = 2 * rows
    count = width // HD // GROUPS
    whole = pltpu.VMEM((rows, width), bf16)
    return pl.pallas_call(
        kernel,
        out_shape=pltpu.VMEM((rows, width), bf16),
        in_specs=[pl.BlockSpec(memory_space=pltpu.SMEM)] * 2
        + [pl.BlockSpec(memory_space=pl.ANY)] * 4,
        out_specs=pl.BlockSpec(memory_space=pltpu.VMEM),
        scratch_shapes=[
            whole,
            pltpu.VMEM((3 * rows, width), bf16),
            pltpu.VMEM((3 * rows, width), bf16),
            whole,
            whole,
            pltpu.VMEM((3 * rows // CHUNK, width, CHUNK), bf16),
            pltpu.VMEM(out_weight.shape, bf16),
            pltpu.VMEM((R, rows), jnp.int32),
            pltpu.VMEM((CHUNK, near), jnp.int32),
            [pltpu.VMEM((CHUNK, width), f32)] * 2,
            [pltpu.VMEM((CHUNK, width), f32)] * 2,
            [pltpu.VMEM((CHUNK, width), f32)] * 2,
            [pltpu.VMEM((CHUNK, near), f32)] * count,
            [pltpu.VMEM((CHUNK, near), bf16)] * count,
            pltpu.VMEM((2 * rows, width), bf16),
            pltpu.VMEM((2 * rows, width), bf16),
            whole,
            whole,
            [pltpu.VMEM((R, rows), f32)] * (2 * G),
            [pltpu.VMEM((R, CHUNK), f32)] * (2 * G),
            [pltpu.VMEM((R, HD), f32)] * (2 * G),
            [pltpu.VMEM((R, HD), f32)] * (2 * G),
            [pltpu.VMEM((R, rows), bf16)] * (2 * G),
            pltpu.VMEM((2 * R, width), f32),
            dma((4,)),
            dma((2, steps)),
            dma((2, steps)),
            dma((2, GROUPS)),
            dma((2, GROUPS)),
            dma((steps, 2)),
            dma((steps, 2)),
            dma((steps,)),
            dma((steps,)),
            dma((steps, PARTS, 2)),
            dma((steps, PARTS)),
        ],
        compiler_params=pltpu.CompilerParams(
            collective_id=0, has_side_effects=True, vmem_limit_bytes=60 << 20
        ),
    )(half_width, valid_length, queries, keys, values, out_weight)


def solution(mesh):
    placed = (
        P(("parts", "seq", "sub"), "heads"),
        P(("parts", "seq", "sub"), "heads"),
        P(("parts", "seq", "sub"), "heads"),
        P(),
        P("parts"),
        P("heads", "sub"),
    )
    return jax.shard_map(
        local,
        mesh=mesh,
        in_specs=placed,
        out_specs=P(("parts", "seq", "sub"), "heads"),
        check_vma=False,
    )
```

```python
import math

import jax
import jax.numpy as jnp
from jax import lax
from jax.experimental import pallas as pl
from jax.experimental.pallas import tpu as pltpu
from jax.sharding import PartitionSpec as P

HD = 128
R = 64
CHUNK = 128
PARTS = 2
G = 2
GROUPS = 4
CLOSED = -1e30
FAR = 1 << 20
EXP2_SCALE = math.log2(math.e) / math.sqrt(HD)
MESH = pl.DeviceIdType.MESH


def kernel(
    half_width,
    valid_length,
    q_hbm,
    k_hbm,
    v_hbm,
    w_hbm,
    out_ref,
    qbuf,
    kbuf,
    vbuf,
    zk,
    zv,
    kt,
    wbuf,
    distance,
    near_distance,
    near_sums,
    near_tops,
    near_totals,
    near_scores,
    near_weights,
    attended,
    terms,
    own_in,
    x_in,
    scores,
    tops,
    totals,
    fixes,
    weights,
    partial,
    local_sem,
    z_send,
    z_recv,
    c_send,
    c_recv,
    a_send,
    a_recv,
    o_send,
    o_recv,
    x_send,
    x_recv,
):
    rows, width = qbuf.shape
    heads_here = width // HD
    steps = rows // R
    own_blocks = rows // CHUNK
    pairs = rows // CHUNK
    lot = width // GROUPS
    cols = width // PARTS
    split = width * 3 // 4
    seq = lax.axis_index("seq")
    group = lax.axis_index("heads")
    sub = lax.axis_index("sub")
    has_z = jnp.where(sub == 0, seq > 0, seq < lax.axis_size("seq") - 1)
    sends_x = sub == 1 - group
    chip_peer = {"sub": 1 - sub}
    z_peer = {"seq": seq + 2 * sub - 1, "sub": 1 - sub}
    first = (seq * 2 + sub) * rows
    length_end = valid_length[0]

    barrier = pltpu.get_barrier_semaphore()
    pl.semaphore_signal(barrier, inc=1, device_id=chip_peer, device_id_type=MESH)
    for core in range(2):
        pl.semaphore_signal(
            barrier, inc=1, device_id={"heads": 1 - group, "sub": core}, device_id_type=MESH
        )

    @pl.when(has_z)
    def _():
        pl.semaphore_signal(barrier, inc=1, device_id=z_peer, device_id_type=MESH)

    own_rows = pl.ds(rows, rows)
    z_rows = pl.ds(pl.multiple_of(2 * rows * sub, rows), rows)
    locals_ = [
        pltpu.make_async_copy(k_hbm, kbuf.at[own_rows], local_sem.at[0]),
        pltpu.make_async_copy(q_hbm, qbuf, local_sem.at[1]),
        pltpu.make_async_copy(v_hbm, vbuf.at[own_rows], local_sem.at[2]),
        pltpu.make_async_copy(w_hbm, wbuf, local_sem.at[3]),
    ]
    for copy in locals_[:3]:
        copy.start()
    kbuf[z_rows, :] = jnp.zeros((rows, width), kbuf.dtype)
    vbuf[z_rows, :] = jnp.zeros((rows, width), vbuf.dtype)
    pl.semaphore_wait(barrier, 3 + has_z.astype(jnp.int32))

    def z_copies(step):
        start = jnp.where(sub == 0, step * R, rows - R - step * R)
        source = pl.ds(pl.multiple_of(start, R), R)
        landing = pl.ds(pl.multiple_of(step * R, R), R)
        return [
            pltpu.make_async_remote_copy(
                src_ref=hbm.at[source],
                dst_ref=buf.at[landing],
                send_sem=z_send.at[which, step],
                recv_sem=z_recv.at[which, step],
                device_id=z_peer,
                device_id_type=MESH,
            )
            for which, (hbm, buf) in enumerate(((k_hbm, zk), (v_hbm, zv)))
        ]

    def c_copies(sender, part):
        at = pl.ds(pl.multiple_of(part * lot, lot), lot)
        landing = (pl.ds(pl.multiple_of(2 * rows * sender, rows), rows), at)
        return [
            pltpu.make_async_remote_copy(
                src_ref=hbm.at[:, at],
                dst_ref=buf.at[landing],
                send_sem=c_send.at[which, part],
                recv_sem=c_recv.at[which, part],
                device_id=chip_peer,
                device_id_type=MESH,
            )
            for which, (hbm, buf) in enumerate(((k_hbm, kbuf), (v_hbm, vbuf)))
        ]

    def a_copy(step, core, half):
        here = (
            pl.ds(pl.multiple_of(2 * R * step + R * core, R), R),
            pl.ds(half * split, (width - split) if half else split),
        )
        return pltpu.make_async_remote_copy(
            src_ref=attended.at[here],
            dst_ref=attended.at[here],
            send_sem=a_send.at[step, half],
            recv_sem=a_recv.at[step, half],
            device_id=chip_peer,
            device_id_type=MESH,
        )

    def o_copy(step):
        return pltpu.make_async_remote_copy(
            src_ref=terms.at[pl.ds(pl.multiple_of(2 * R * step + R * (1 - sub), R), R)],
            dst_ref=own_in.at[pl.ds(pl.multiple_of(R * step, R), R)],
            send_sem=o_send.at[step],
            recv_sem=o_recv.at[step],
            device_id=chip_peer,
            device_id_type=MESH,
        )

    def x_copy(step, part, core):
        at = pl.ds(part * cols, cols)
        return pltpu.make_async_remote_copy(
            src_ref=terms.at[pl.ds(pl.multiple_of(2 * R * step + R * core, R), R), at],
            dst_ref=x_in.at[pl.ds(pl.multiple_of(R * step, R), R), at],
            send_sem=x_send.at[step, part, core],
            recv_sem=x_recv.at[step, part],
            device_id={"heads": 1 - group, "sub": core},
            device_id_type=MESH,
        )

    def send_z(begin, end):
        @pl.when(has_z)
        def _():
            for step in range(begin, end):
                for copy in z_copies(step):
                    copy.start()

    send_z(0, 1)
    for part in range(GROUPS):
        for copy in c_copies(sub, part):
            copy.start()
    send_z(1, steps)

    def turn(block, head):
        source = pl.ds(pl.multiple_of(block * CHUNK, CHUNK), CHUNK)
        lanes = pl.ds(pl.multiple_of(head * HD, HD), HD)
        kt[block, lanes, :] = kbuf[source, lanes].T

    def query_row(step):
        return pl.multiple_of(jnp.where(sub == 0, rows - R - step * R, step * R), R)

    locals_[0].wait()

    def turn_own(head, carry):
        for block in range(own_blocks):
            turn(own_blocks + block, head)
        return carry

    lax.fori_loop(0, heads_here, turn_own, 0)
    for copy in locals_[1:3]:
        copy.wait()
    locals_[3].start()

    def finish(step):
        for part in range(PARTS):
            x_copy(step, part, 0).wait_recv()
        here = pl.ds(pl.multiple_of(R * step, R), R)
        target = pl.ds(query_row(step), R)

        def add(own):
            out_ref[target, :] = (own.astype(jnp.float32) + x_in[here, :].astype(jnp.float32)).astype(
                out_ref.dtype
            )

        @pl.when(sends_x)
        def _():
            o_copy(step).wait_recv()
            add(own_in[here, :])

        @pl.when(jnp.logical_not(sends_x))
        def _():
            add(terms[pl.ds(pl.multiple_of(2 * R * step + R * sub, R), R), :])

    def near_place(pair):
        row = pl.multiple_of(jnp.where(sub == 0, rows - CHUNK - pair * CHUNK, pair * CHUNK), CHUNK)
        return row, jnp.where(sub == 0, own_blocks, pair)

    def keys_fine(key_pos):
        return (key_pos >= 0) & (key_pos < length_end)

    def near_masks(pair):
        row, block = near_place(pair)
        span = (2 * own_blocks - pair) * CHUNK
        row_at = lax.broadcasted_iota(jnp.int32, (CHUNK, span), 0) + (rows + row)
        key_at = lax.broadcasted_iota(jnp.int32, (CHUNK, span), 1) + block * CHUNK
        near_distance[:, :span] = jnp.where(
            keys_fine(key_at + (first - rows)), jnp.abs(row_at - key_at), FAR
        )

    def near_group(pair, part):
        row, first_block = near_place(pair)
        blocks = 2 * own_blocks - pair
        span = blocks * CHUNK
        keys_here = pl.ds(pl.multiple_of(first_block * CHUNK, CHUNK), span)
        queries_here = pl.ds(row, CHUNK)
        side = pair % 2
        count = heads_here // GROUPS
        lanes_of = [
            pl.ds(pl.multiple_of((part * count + one) * HD, HD), HD) for one in range(count)
        ]
        for one, lanes in enumerate(lanes_of):
            block_keys = jnp.concatenate(
                [kt[first_block + block, lanes, :] for block in range(blocks)], axis=1
            )
            raw = jnp.dot(qbuf[queries_here, lanes], block_keys, preferred_element_type=jnp.float32)
            wide = half_width[group * heads_here + part * count + one]
            raw = jnp.where(near_distance[:, :span] <= wide, raw, CLOSED)
            near_scores[one][:, :span] = raw
            top = raw[:, :CHUNK]
            for block in range(1, blocks):
                top = jnp.maximum(top, raw[:, block * CHUNK : (block + 1) * CHUNK])
            near_tops[side][:, lanes] = jnp.broadcast_to(
                jnp.max(top, axis=1, keepdims=True), (CHUNK, HD)
            )
        for one, lanes in enumerate(lanes_of):
            top = near_tops[side][:, lanes]
            total = jnp.zeros((CHUNK, HD), jnp.float32)
            for block in range(blocks):
                at = pl.ds(block * CHUNK, CHUNK)
                exact = jnp.exp2((near_scores[one][:, at] - top) * EXP2_SCALE)
                total = total + exact
                near_weights[one][:, at] = exact.astype(jnp.bfloat16)
            near_totals[side][:, lanes] = jnp.broadcast_to(
                jnp.sum(total, axis=1, keepdims=True), (CHUNK, HD)
            )
        for one, lanes in enumerate(lanes_of):
            near_sums[side][:, lanes] = jnp.dot(
                near_weights[one][:, :span],
                vbuf[keys_here, lanes],
                preferred_element_type=jnp.float32,
            )

    def first_group(part, carry):
        for copy in c_copies(1 - sub, part):
            copy.wait_recv()
        count = heads_here // GROUPS
        for one in range(count):
            for block in range(own_blocks):
                turn(2 * own_blocks * (1 - sub) + block, part * count + one)
        near_group(0, part)
        return carry

    def near_groups(pair, begin, count):
        lax.fori_loop(0, count, lambda i, c: (near_group(pair, begin + i), c)[1], 0)

    def far_step(pair, step):
        row = query_row(step)
        queries_here = pl.ds(row, R)
        first_block = jnp.where(sub == 0, own_blocks - 1 - pair, 2 * own_blocks)
        blocks = pair + 1
        span = blocks * CHUNK
        keys_here = pl.ds(pl.multiple_of(first_block * CHUNK, CHUNK), span)
        side = pair % 2
        half = step % 2
        near_rows = pl.ds(pl.multiple_of(R * jnp.where(sub == 0, 1 - half, half), R), R)

        row_at = lax.broadcasted_iota(jnp.int32, (R, span), 0) + (rows + row)
        key_at = lax.broadcasted_iota(jnp.int32, (R, span), 1) + first_block * CHUNK
        distance[:, :span] = jnp.where(
            keys_fine(key_at + (first - rows)), jnp.abs(row_at - key_at), FAR
        )
        row_fine = (lax.broadcasted_iota(jnp.int32, (R, HD), 0) + (first + row)) < length_end
        done = pl.ds(pl.multiple_of(2 * R * step + R * sub, R), R)

        @pl.when(has_z)
        def _():
            for copy in z_copies(step):
                copy.wait_recv()
            landed = pl.ds(pl.multiple_of(step * R, R), R)
            start = jnp.where(sub == 0, row, 2 * rows + row)
            place = pl.ds(pl.multiple_of(start, R), R)
            kbuf[place, :] = zk[landed, :]
            vbuf[place, :] = zv[landed, :]
            for head in range(heads_here):
                turn(start // CHUNK, head)

        def score(head, slot):
            lanes = pl.ds(head * HD, HD)
            block_keys = jnp.concatenate(
                [kt[first_block + block, lanes, :] for block in range(blocks)], axis=1
            )
            raw = jnp.dot(qbuf[queries_here, lanes], block_keys, preferred_element_type=jnp.float32)
            wide = half_width[group * heads_here + head]
            raw = jnp.where(distance[:, :span] <= wide, raw, CLOSED)
            scores[slot][:, :span] = raw
            top = raw[:, :CHUNK]
            for block in range(1, blocks):
                top = jnp.maximum(top, raw[:, block * CHUNK : (block + 1) * CHUNK])
            top = jnp.broadcast_to(jnp.max(top, axis=1, keepdims=True), (R, HD))
            tops[slot][...] = jnp.maximum(top, near_tops[side][near_rows, lanes])

        def weigh(head, slot):
            lanes = pl.ds(head * HD, HD)
            top = tops[slot][...]
            fixes[slot][...] = jnp.exp2((near_tops[side][near_rows, lanes] - top) * EXP2_SCALE)
            total = jnp.zeros((R, CHUNK), jnp.float32)
            for block in range(blocks):
                at = pl.ds(block * CHUNK, CHUNK)
                exact = jnp.exp2((scores[slot][:, at] - top) * EXP2_SCALE)
                total = total + exact
                weights[slot][:, at] = exact.astype(jnp.bfloat16)
            totals[slot][...] = jnp.broadcast_to(jnp.sum(total, axis=1, keepdims=True), (R, HD))

        def gather(head, slot):
            lanes = pl.ds(head * HD, HD)
            fix = fixes[slot][...]
            sums = near_sums[side][near_rows, lanes] * fix + jnp.dot(
                weights[slot][:, :span], vbuf[keys_here, lanes], preferred_element_type=jnp.float32
            )
            total = near_totals[side][near_rows, lanes] * fix + totals[slot][...]
            attended[done, lanes] = jnp.where(row_fine, sums / total, 0.0).astype(attended.dtype)

        stages = heads_here // G
        for stage in range(stages + 2):
            for one in range(G):
                if stage < stages:
                    score(stage * G + one, stage % 2 * G + one)
                if 1 <= stage <= stages:
                    weigh((stage - 1) * G + one, (stage - 1) % 2 * G + one)
                if stage >= 2:
                    gather((stage - 2) * G + one, stage % 2 * G + one)
            if (stage - 1) * G * HD == split:
                a_copy(step, sub, 0).start()
        a_copy(step, sub, 1).start()

    early, late = (pl.ds(0, split), pl.ds(split, width - split))

    def project_early(step):
        both = pl.ds(pl.multiple_of(2 * R * step, 2 * R), 2 * R)
        a_copy(step, 1 - sub, 0).wait_recv()
        for part in range(PARTS):
            at = pl.ds(part * cols, cols)
            partial[:, at] = jnp.dot(
                attended[both, early], wbuf[early, at], preferred_element_type=jnp.float32
            )
        a_copy(step, 1 - sub, 1).wait_recv()

    def project(step, begun):
        both = pl.ds(pl.multiple_of(2 * R * step, 2 * R), 2 * R)
        if begun:
            project_early(step)
        else:
            for half in range(2):
                a_copy(step, 1 - sub, half).wait_recv()
        for part in range(PARTS):
            at = pl.ds(part * cols, cols)
            if begun:
                shares = partial[:, at] + jnp.dot(
                    attended[both, late], wbuf[late, at], preferred_element_type=jnp.float32
                )
            else:
                shares = jnp.dot(attended[both, :], wbuf[:, at], preferred_element_type=jnp.float32)
            terms[both, at] = shares.astype(terms.dtype)

            @pl.when(sends_x)
            def _():
                for core in range(2):
                    x_copy(step, part, core).start()

        @pl.when(jnp.logical_not(sends_x))
        def _():
            o_copy(step).start()

    near_masks(0)
    lax.fori_loop(0, GROUPS, first_group, 0)
    far_step(0, 0)
    locals_[3].wait()
    project(0, True)
    near_masks(1)
    near_groups(1, 0, GROUPS // 2)
    far_step(0, 1)
    near_groups(1, GROUPS // 2, GROUPS // 2)
    project(1, False)

    for pair in range(1, pairs):
        more = pair + 1 < pairs
        if more:
            near_masks(pair + 1)

        def in_pair(half, carry):
            step = 2 * pair + half
            far_step(pair, step)
            if more:
                near_groups(pair + 1, half * (GROUPS // 2), GROUPS // 2)
            if not more:
                finish(step - 2)
            project(step, not more)
            if more:
                finish(step - 2)
            return carry

        lax.fori_loop(0, 2, in_pair, 0)
    for part in range(GROUPS):
        for copy in c_copies(sub, part):
            copy.wait_send()
    for step in range(steps):
        for half in range(2):
            a_copy(step, sub, half).wait_send()

    @pl.when(has_z)
    def _():
        for step in range(steps):
            for copy in z_copies(step):
                copy.wait_send()

    def sent(begin, end):
        @pl.when(sends_x)
        def _():
            for step in range(begin, end):
                for part in range(PARTS):
                    for core in range(2):
                        x_copy(step, part, core).wait_send()

        @pl.when(jnp.logical_not(sends_x))
        def _():
            for step in range(begin, end):
                o_copy(step).wait_send()

    sent(0, steps - 2)
    finish(steps - 2)
    sent(steps - 2, steps - 1)
    finish(steps - 1)
    sent(steps - 1, steps)


def local(queries, keys, values, half_width, valid_length, out_weight):
    rows, width = queries.shape
    bf16, f32 = jnp.bfloat16, jnp.float32
    dma = pltpu.SemaphoreType.DMA
    steps = rows // R
    near = 2 * rows
    count = width // HD // GROUPS
    whole = pltpu.VMEM((rows, width), bf16)
    return pl.pallas_call(
        kernel,
        out_shape=pltpu.VMEM((rows, width), bf16),
        in_specs=[pl.BlockSpec(memory_space=pltpu.SMEM)] * 2
        + [pl.BlockSpec(memory_space=pl.ANY)] * 4,
        out_specs=pl.BlockSpec(memory_space=pltpu.VMEM),
        scratch_shapes=[
            whole,
            pltpu.VMEM((3 * rows, width), bf16),
            pltpu.VMEM((3 * rows, width), bf16),
            whole,
            whole,
            pltpu.VMEM((3 * rows // CHUNK, width, CHUNK), bf16),
            pltpu.VMEM(out_weight.shape, bf16),
            pltpu.VMEM((R, rows), jnp.int32),
            pltpu.VMEM((CHUNK, near), jnp.int32),
            [pltpu.VMEM((CHUNK, width), f32)] * 2,
            [pltpu.VMEM((CHUNK, width), f32)] * 2,
            [pltpu.VMEM((CHUNK, width), f32)] * 2,
            [pltpu.VMEM((CHUNK, near), f32)] * count,
            [pltpu.VMEM((CHUNK, near), bf16)] * count,
            pltpu.VMEM((2 * rows, width), bf16),
            pltpu.VMEM((2 * rows, width), bf16),
            whole,
            whole,
            [pltpu.VMEM((R, rows), f32)] * (2 * G),
            [pltpu.VMEM((R, CHUNK), f32)] * (2 * G),
            [pltpu.VMEM((R, HD), f32)] * (2 * G),
            [pltpu.VMEM((R, HD), f32)] * (2 * G),
            [pltpu.VMEM((R, rows), bf16)] * (2 * G),
            pltpu.VMEM((2 * R, width), f32),
            dma((4,)),
            dma((2, steps)),
            dma((2, steps)),
            dma((2, GROUPS)),
            dma((2, GROUPS)),
            dma((steps, 2)),
            dma((steps, 2)),
            dma((steps,)),
            dma((steps,)),
            dma((steps, PARTS, 2)),
            dma((steps, PARTS)),
        ],
        compiler_params=pltpu.CompilerParams(
            collective_id=0, has_side_effects=True, vmem_limit_bytes=60 << 20
        ),
    )(half_width, valid_length, queries, keys, values, out_weight)


def solution(mesh):
    placed = (
        P(("parts", "seq", "sub"), "heads"),
        P(("parts", "seq", "sub"), "heads"),
        P(("parts", "seq", "sub"), "heads"),
        P(),
        P("parts"),
        P("heads", "sub"),
    )
    return jax.shard_map(
        local,
        mesh=mesh,
        in_specs=placed,
        out_specs=P(("parts", "seq", "sub"), "heads"),
        check_vma=False,
    )
```
